32 devices in a mesh: rows: 4 (over x, core), cols: 8 (over z, y).
Axes of the slice: x: 2, y: 2, z: 4, core: 2. Of those that a mesh axis runs over, the one named last changes fastest.
Arguments:
- pair_integrals: float32 [4096, 4096], P('rows', 'cols'), may hold values from -6 to 6
- left_factor: float32 [4096, 1024], P('rows', 'cols'), may hold values from -0.9375 to 0.9375
- core: float32 [1024, 1024], replicated, may hold values from -6 to 6
- right_factor: float32 [4096, 1024], P('cols', 'rows'), may hold values from -0.9375 to 0.9375
Outputs:
- core_next: float32 [1024, 1024], replicated
The draws below stay inside these ranges and needn't reach their ends.
All inputs are finite; a program needn't handle non-finite values.
Results may differ from the reference program's by a relative error of at most 0.000062.
Values sent between devices are 32-bit elements; how exact they have to be, the bound alone decides.
No kernel may reach another device: no remote copies, remote signals or barrier semaphores. Data moves between devices by JAX's collectives and lax.ppermute only.
A program may use at most 128 MiB of HBM per device.

```python
import math
import jax
import jax.numpy as jnp
from jax import lax

RANK = 1024
PAIRS_ROW = 4096
PAIRS_COL = 4096


def factor_draw(base_key, row_count, salt_value):
    base_key = jax.random.fold_in(base_key, salt_value)
    key_entries, key_scale = jax.random.split(base_key, 2)
    entries = jax.random.truncated_normal(key_entries, -4.0, 4.0, (row_count, RANK), jnp.float32)
    rise_total = 3.5
    row_scale = jnp.exp(jax.random.uniform(key_scale, (row_count, 1), jnp.float32, math.log(0.2), math.log(0.8)))
    position = jnp.arange(row_count, dtype=jnp.float32).reshape(row_count, 1) / float(max(row_count - 1, 1))
    rising = jnp.exp(math.log(rise_total) * position)
    return entries * row_scale * rising / math.sqrt(row_count)


def draw_left_factor(key, part):
    return factor_draw(key, PAIRS_ROW, 101)


def draw_right_factor(key, part):
    return factor_draw(key, PAIRS_COL, 202)


def shard_levels(stream_key, shape, cuts, least, largest):
    gain = 1.0
    for dim, shards_of in cuts:
        steps = jax.random.uniform(jax.random.fold_in(jax.random.fold_in(stream_key, 6), dim), (shards_of,), jnp.float32, least / len(cuts), largest / len(cuts))
        gain = gain * jnp.repeat(jnp.exp(steps), shape[dim] // shards_of).reshape((-1,) + (1,) * (len(shape) - 1 - dim))
    return gain


def bell_draw(own_key, extent, spread, limit, shards=(), held_as=jnp.bfloat16):
    values = jax.random.normal(own_key, extent, jnp.float32) * spread
    if len(shards) > 0:
        values = shard_levels(own_key, extent, shards, -0.22, 0.18) * values
    return jnp.clip(values, min=-limit, max=limit).astype(held_as)


def setup_inputs(seed: int = 0) -> dict:
    key_of = jax.random.split(jax.random.key(seed), 5)
    return {
        "pair_integrals": bell_draw(key_of[0], (PAIRS_ROW, PAIRS_COL), 1.0, 6.0, ((0, 4), (1, 8)), jnp.float32),
        "left_factor": draw_left_factor(jax.random.fold_in(key_of[4], 71), 0),
        "core": bell_draw(key_of[2], (RANK, RANK), 1.0, 6.0, (), jnp.float32),
        "right_factor": draw_right_factor(jax.random.fold_in(key_of[4], 71), 0),
    }


def reference(pair_integrals, left_factor, core, right_factor):
    highest = lax.Precision.HIGHEST
    mixed = jnp.dot(core, right_factor.T, precision=highest, preferred_element_type=jnp.float32)
    residual = pair_integrals - jnp.dot(left_factor, mixed, precision=highest, preferred_element_type=jnp.float32)
    along = jnp.dot(residual, right_factor, precision=highest, preferred_element_type=jnp.float32)
    gradient = jnp.dot(left_factor.T, along, precision=highest, preferred_element_type=jnp.float32)
    numer = jnp.sum(gradient * gradient)
    inner = jnp.dot(gradient, right_factor.T, precision=highest, preferred_element_type=jnp.float32)
    image = jnp.dot(left_factor, inner, precision=highest, preferred_element_type=jnp.float32)
    denom = jnp.sum(image * image)
    return core + (numer / denom) * gradient
```

```python
import jax
import jax.numpy as jnp
from jax import lax
from jax.sharding import PartitionSpec as P


def dot(left, right, contract):
    return lax.dot_general(
        left,
        right,
        (contract, ((), ())),
        precision=lax.Precision.HIGH,
        preferred_element_type=jnp.float32,
    )


def pick(array, index, axis):
    return lax.dynamic_index_in_dim(array, index, axis, keepdims=False)


def solution(mesh):
    rows, cols = mesh.shape["rows"], mesh.shape["cols"]
    nx, nz = rows // 2, cols // 2

    def swap_core(a):
        return lax.ppermute(a, "rows", [(i, i ^ 1) for i in range(rows)])

    def shift_x(a, d):
        return lax.ppermute(a, "rows", [(i, (i + 2 * d) % rows) for i in range(rows)])

    def swap_y(a):
        return lax.ppermute(a, "cols", [(i, i ^ 1) for i in range(cols)])

    def shift_z(a, d):
        return lax.ppermute(a, "cols", [(i, (i + 2 * d) % cols) for i in range(cols)])

    def shards(pair_integrals, left_factor, core, right_factor):
        row, col = lax.axis_index("rows"), lax.axis_index("cols")
        x, c, z, y = row // 2, row % 2, col // 2, col % 2
        rank = core.shape[0]
        height, block = left_factor.shape
        width, part = right_factor.shape
        sub = block // rows

        left_t = jnp.zeros((nz, 2, block, height), jnp.float32)
        held = left_factor.T
        for d in range(nz):
            if d > 0:
                held = shift_z(held, 1)
            other = swap_y(held)
            at = (z - d) % nz
            left_t = lax.dynamic_update_slice(left_t, held[None, None], (at, y, 0, 0))
            left_t = lax.dynamic_update_slice(left_t, other[None, None], (at, 1 - y, 0, 0))
        left_t = left_t.reshape(rank, height)

        blocks = {}
        for d in range(nx):
            mine = right_factor if d == 0 else shift_x(right_factor, d)
            blocks[d, 0], blocks[d, 1] = mine, swap_core(mine)
        ordered = []
        for i in range(nx):
            for j in range(2):
                one = blocks[0, 0]
                for d in range(nx):
                    for e in range(2):
                        hit = ((x - d) % nx == i) & (c ^ e == j)
                        one = jnp.where(hit, blocks[d, e], one)
                ordered.append(one)
        right = jnp.concatenate(ordered, axis=1)

        mixed = dot(core, right, ((1,), (1,)))
        residual = pair_integrals - dot(left_t, mixed, ((0,), (0,)))
        across = dot(left_t, residual, ((1,), (0,))).reshape(nz, 2, nx, 2, sub, width)

        across = pick(across, c, 3) + swap_core(pick(across, 1 - c, 3))
        total = pick(across, x, 2)
        for d in range(1, nx):
            total = total + shift_x(pick(across, (x + d) % nx, 2), d)

        term = dot(total.reshape(nz * 2 * sub, width), right, ((1,), (0,)))
        term = term.reshape(nz, 2, sub, rank)
        term = pick(term, y, 1) + swap_y(pick(term, 1 - y, 1))
        own = pick(term, z, 0)
        for d in range(1, nz):
            own = own + shift_z(pick(term, (z + d) % nz, 0), d)
        numer = jnp.sum(own * own)

        line = jnp.zeros((nz, sub, rank), jnp.float32)
        for d in range(nz):
            piece = own if d == 0 else shift_z(own, d)
            line = lax.dynamic_update_slice(line, piece[None], ((z - d) % nz, 0, 0))
        half = nz // 2
        first, second = line[:half], line[half:]
        first = {0: first, 1: swap_y(first)}
        second = {(0, d): second if d == 0 else shift_x(second, d) for d in range(nx)}
        pieces = []
        joined = jnp.concatenate([first[0], first[1]])
        for d in range(nx):
            got = joined if d == 0 else shift_x(joined, d)
            pieces.append((0, 0, d, got[:half]))
            pieces.append((0, 1, d, got[half:]))
        joined = jnp.concatenate([second[0, d] for d in range(nx)])
        got = swap_y(joined)
        for d in range(nx):
            pieces.append((half, 0, d, second[0, d]))
            pieces.append((half, 1, d, got[d * half:(d + 1) * half]))
        gradient = jnp.zeros((nz, 2, nx, 2, sub, rank), jnp.float32)
        for start, e, d, value in pieces:
            for f in range(2):
                value = value if f == 0 else swap_core(value)
                gradient = lax.dynamic_update_slice(
                    gradient,
                    value[:, None, None, None],
                    (start, y ^ e, (x - d) % nx, c ^ f, 0, 0),
                )
        gradient = gradient.reshape(rank, rank)

        inner = dot(gradient, right, ((1,), (1,)))
        image = dot(left_t, inner, ((0,), (0,)))
        sums = jnp.stack([numer, jnp.sum(image * image)]).reshape(1, 2)
        sums = sums + swap_core(sums)
        sums = sum((shift_x(sums, d) for d in range(1, nx)), sums)
        sums = sums + swap_y(sums)
        step = 1
        while step < nz:
            sums = sums + shift_z(sums, step)
            step *= 2
        return core + sums[0, 0] / sums[0, 1] * gradient

    return jax.shard_map(
        shards,
        mesh=mesh,
        in_specs=(P("rows", "cols"), P("rows", "cols"), P(), P("cols", "rows")),
        out_specs=P(),
        check_vma=False,
    )
```
